32 devices in a mesh: space: 8 (over z, x), snap: 4 (over y, core).
Axes of the slice: x: 2, y: 2, z: 4, core: 2. Of those that a mesh axis runs over, the one named last changes fastest.
Arguments:
- snapshots: bfloat16 [131072, 512], P('space', 'snap'), may hold values from -6 to 6
- mass_blocks: bfloat16 [1024, 3, 128, 128], P(('space', 'snap')), may hold values from -0.3125 to 0.3125
- neighbours: int32 [1024, 3], P(('space', 'snap')), may hold values from 0 to 1023, as said below
- eigvecs: bfloat16 [512, 128], replicated, may hold values from -0.25 to 0.25
Outputs:
- weighted: bfloat16 [131072, 512], P(('space', 'snap'))
- correlation: float32 [512, 512], P('snap', 'space')
- modes: bfloat16 [131072, 128], P(('space', 'snap'))
The draws below stay inside these ranges and needn't reach their ends.
Inputs may be any that keep to these rules, and one draw needn't show every extreme that they name: neighbours[b, 0] is b; every entry lies within 4 of b; neighbours[b, 2] lies exactly 4 away from b.
All inputs are finite; a program needn't handle non-finite values.
Results may differ from the reference program's by a relative error of at most 0.0029.
Values may be sent and summed in bfloat16 or wider, within the bound.
A program may use at most 128 MiB of HBM per device.

```python
import jax
import jax.numpy as jnp
from jax import lax

SNAPS = 512
MODES = 128
BLOCK = 128
NB = 3
HB = 4
NCELLS = 131072
NBLK = 1024


def draw_neighbours(key, part):
    block_ids = jnp.arange(NBLK, dtype=jnp.int32)
    key_one, key_two, key_three = jax.random.split(key, 3)
    reach_one = jax.random.randint(key_one, (NBLK,), 1, HB + 1, dtype=jnp.int32)
    sign_one = jax.random.randint(key_two, (NBLK,), 0, 2, dtype=jnp.int32) * 2 - 1
    sign_two = jax.random.randint(key_three, (NBLK,), 0, 2, dtype=jnp.int32) * 2 - 1

    def mirror(reach, sign):
        target = block_ids + sign * reach
        outside = (target < 0) | (target >= NBLK)
        return jnp.where(outside, block_ids - sign * reach, target)
    far_reach = jnp.full((NBLK,), HB, dtype=jnp.int32)
    return jnp.stack([block_ids, mirror(reach_one, sign_one), mirror(far_reach, sign_two)], axis=1).astype(jnp.int32)


def block_levels(stream_key, extent, cuts, smallest, largest):
    level, own = 1.0, jax.random.fold_in(stream_key, 6)
    for position, blocks in cuts:
        draws = jnp.exp(jax.random.uniform(jax.random.fold_in(own, position), (blocks,), jnp.float32, smallest / len(cuts), largest / len(cuts)))
        level = level * jnp.repeat(draws, extent[position] // blocks).reshape([-1 if axis == position else 1 for axis in range(len(extent))])
    return level


def bell_draw(rng, dims, spread, bound, cuts=(), kind=jnp.bfloat16):
    result = spread * jax.random.normal(rng, dims, jnp.float32)
    if cuts:
        result = result * block_levels(rng, dims, cuts, -0.22, 0.18)
    return jnp.clip(result, -bound, bound).astype(kind)


def setup_inputs(seed: int = 0) -> dict:
    seeds = jax.random.split(jax.random.key(seed), 5)
    snapshots = bell_draw(seeds[0], (NCELLS, SNAPS), 1.0, 6.0, ((0, 8), (1, 4)))
    mass_blocks = bell_draw(seeds[1], (NBLK, NB, BLOCK, BLOCK), (NB * BLOCK) ** -0.5, 0.3125, ((0, 32),))
    neighbours = draw_neighbours(jax.random.fold_in(seeds[4], 71), 0)
    eigvecs = bell_draw(seeds[3], (SNAPS, MODES), SNAPS ** -0.5, 0.25)
    return dict(snapshots=snapshots, mass_blocks=mass_blocks, neighbours=neighbours, eigvecs=eigvecs)


group_size = 32


def reference(snapshots, mass_blocks, neighbours, eigvecs):
    blocks = snapshots.reshape(NBLK, BLOCK, SNAPS)

    def weigh(packed):
        mass_part, block_ids = packed
        nearby = blocks[block_ids].astype(jnp.float32)
        return jnp.einsum("bjrc,bjcs->brs", mass_part.astype(jnp.float32), nearby)

    stacked = lax.map(weigh, (mass_blocks.reshape(-1, group_size, NB, BLOCK, BLOCK), neighbours.reshape(-1, group_size, NB)))
    weighted = stacked.reshape(NCELLS, SNAPS).astype(jnp.bfloat16)
    correlation = jnp.dot(weighted.T, snapshots, preferred_element_type=jnp.float32) * (1.0 / NCELLS)
    modes = jnp.dot(snapshots, eigvecs, preferred_element_type=jnp.float32).astype(jnp.bfloat16)
    return weighted, correlation, modes
```

```python
import functools

import jax
import jax.numpy as jnp
from jax import lax
from jax.experimental import pallas as pl
from jax.experimental.pallas import tpu as pltpu
from jax.sharding import PartitionSpec as P

HB = 4
MESH = pl.DeviceIdType.MESH
BF16 = jnp.bfloat16
F32 = jnp.float32


def exchange(n, ns, rim, src, ext, bounce, rim_bounce, loc, rim_loc, send_own, recv_own,
             send_mid, recv_mid, send_main, recv_main, send_fwd, recv_fwd,
             send_rim, recv_rim, send_out):
    ny = n // 2
    s, k = lax.axis_index("space"), lax.axis_index("snap")
    y, c = k // 2, k % 2
    partner = 2 * y + 1 - c
    total = src.shape[0]
    chip_rows = total // ny
    rows = chip_rows // 2
    part = rows - rim

    barrier = pltpu.get_barrier_semaphore()
    for t in range(1, n):
        pl.semaphore_signal(barrier, inc=1, device_id=(s, lax.rem(k + t, n)), device_id_type=MESH)

    @pl.when(s > 0)
    def _():
        for t in range(n):
            pl.semaphore_signal(barrier, inc=1, device_id=(s - 1, t), device_id_type=MESH)

    @pl.when(s < ns - 1)
    def _():
        for t in range(n):
            pl.semaphore_signal(barrier, inc=1, device_id=(s + 1, t), device_id_type=MESH)

    load = pltpu.make_async_copy(src.at[pl.ds(y * chip_rows + c * part, rows + rim)], bounce, loc.at[0])
    load.start()
    sides = jnp.where(s > 0, 1, 0) + jnp.where(s < ns - 1, 1, 0)
    pl.semaphore_wait(barrier, n - 1 + n * sides)

    def remote(origin, slab, to_row, count, sends, recvs, device):
        return pltpu.make_async_remote_copy(
            src_ref=origin, dst_ref=ext.at[slab, pl.ds(to_row, count)],
            send_sem=sends, recv_sem=recvs, device_id=device, device_id_type=MESH)

    def rows_of(first, count):
        return src.at[pl.ds(first, count)]

    mids, mains = [], []
    for t in range(1, ny):
        yo = lax.rem(y + t, ny)
        base = yo * chip_rows
        for co in range(2):
            target = (s, 2 * yo + co)
            mids.append(remote(rows_of(base + part + co * rim, rim), k, rows if co == 0 else rim, rim,
                               send_mid.at[t, co], recv_mid.at[t, c], target))
            mains.append(remote(rows_of(base if co == 0 else base + rows + rim, part), k,
                                rim if co == 0 else 2 * rim, part,
                                send_main.at[t, co], recv_main.at[t, c], target))
    own = remote(rows_of(y * chip_rows + (1 - c) * part, rows + rim), k, c * rim, rows + rim,
                 send_own, recv_own, (s, partner))
    down = remote(rows_of(0, rim), k, rows + rim, rim, send_out.at[0], recv_rim.at[k], (s - 1, n - 1))
    up = remote(rows_of(total - rim, rim), k, 0, rim, send_out.at[1], recv_rim.at[k], (s + 1, 0))

    for copy in mids:
        copy.start()
    pl.when(s > 0)(down.start)
    pl.when(s < ns - 1)(up.start)
    edges = []
    for target in range(1, n - 1):
        low = target % 2 == 0
        first = (target // 2) * chip_rows - rim if low else (target // 2 + 1) * chip_rows
        edge = remote(rows_of(first, rim), k, 0 if low else rows + rim, rim,
                      send_rim.at[target], recv_rim.at[k], (s, target))
        edges.append((target, edge))
        pl.when(k != target)(edge.start)
    own.start()
    for copy in mains:
        copy.start()

    load.wait()
    keep = pltpu.make_async_copy(bounce, ext.at[k, pl.ds((1 - c) * rim, rows + rim)], loc.at[1])
    keep.start()
    inner = (k > 0) & (k < n - 1)
    edge_row = jnp.where(c == 0, y * chip_rows - rim, (y + 1) * chip_rows)
    edge_row = jnp.where(inner, edge_row, 0)

    @pl.when(inner)
    def _():
        take = pltpu.make_async_copy(rows_of(edge_row, rim), rim_bounce, rim_loc.at[0])
        take.start()
        take.wait()
        put = pltpu.make_async_copy(rim_bounce, ext.at[k, pl.ds(c * (rows + rim), rim)], rim_loc.at[1])
        put.start()
        put.wait()

    forwards = []
    for t in range(1, ny):
        yo = lax.rem(y + ny - t, ny)
        for co in range(2):
            slab = 2 * yo + co
            at = (1 - c) * rows + c * rim
            held = ext.at[slab, pl.ds(at, rim)]
            remote(held, slab, at, rim, send_mid.at[t, co], recv_mid.at[t, co], (s, partner)).wait_recv()
            forward = remote(held, slab, c * (rows + rim), rim,
                             send_fwd.at[t, co], recv_fwd.at[t, co], (s, partner))
            forward.start()
            forwards.append((slab, t, co, forward))

    own_slab = partner
    remote(ext.at[own_slab, pl.ds(0, rows + rim)], own_slab, (1 - c) * rim, rows + rim,
           send_own, recv_own, (s, partner)).wait_recv()
    lowest = (k == 0) & (s == 0)
    highest = (k == n - 1) & (s == ns - 1)
    for slab in range(n):
        rim_at = ext.at[slab, pl.ds(c * (rows + rim), rim)]
        expected = jnp.logical_not(lowest | highest | (inner & (k == slab)))

        @pl.when(expected)
        def _(rim_at=rim_at, slab=slab):
            remote(rim_at, slab, c * (rows + rim), rim, send_rim.at[0], recv_rim.at[slab],
                   (s, partner)).wait_recv()
    for slab, t, co, forward in forwards:
        to = (1 - c) * (rows + rim)
        remote(ext.at[slab, pl.ds(to, rim)], slab, to, rim, send_fwd.at[t, co], recv_fwd.at[t, co],
               (s, partner)).wait_recv()
        at = rim + c * rim
        remote(ext.at[slab, pl.ds(at, part)], slab, at, part, send_main.at[t, co], recv_main.at[t, co],
               (s, partner)).wait_recv()

    keep.wait()
    for copy in mids + mains + [own] + [entry[3] for entry in forwards]:
        copy.wait_send()
    pl.when(s > 0)(down.wait_send)
    pl.when(s < ns - 1)(up.wait_send)
    for target, edge in edges:
        pl.when(k != target)(edge.wait_send)


def compute(n, per_step, near, ext, mass, eig, weighted, modes, corr):
    step = pl.program_id(0)
    size = mass.shape[2]

    @pl.when(step == 0)
    def _():
        corr[...] = jnp.zeros_like(corr)

    def block_at(index):
        first = pl.multiple_of(index * size, size)
        return jnp.concatenate([ext[slab, pl.ds(first, size), :] for slab in range(n)], axis=1)

    for local in range(per_step):
        row = step * per_step + local
        masses = jnp.concatenate([mass[local, j] for j in range(mass.shape[1])], axis=1)
        fields = jnp.concatenate([block_at(near[row, j]) for j in range(mass.shape[1])], axis=0)
        product = jnp.dot(masses, fields, preferred_element_type=F32)
        weighted[pl.ds(local * size, size), :] = product.astype(BF16)
    first = pl.multiple_of((step * per_step + HB) * size, size)
    here = jnp.concatenate([ext[slab, pl.ds(first, per_step * size), :] for slab in range(n)], axis=1)
    modes[...] = jnp.dot(here, eig[...], preferred_element_type=F32).astype(BF16)
    sums = lax.dot_general(here, weighted[...], (((0,), (0,)), ((), ())), preferred_element_type=F32)
    width = corr.shape[2]
    for band in range(n):
        corr[band] += sums[:, band * width:(band + 1) * width]


def reduce_kernel(n, ns, scale, part, out, recv1, send2, recv2, send3, recv3, send4, recv4,
                  s1, r1, s2, r2, s3, r3, s4, r4):
    ny, nz = n // 2, ns // 2
    s, k = lax.axis_index("space"), lax.axis_index("snap")
    y, c, z, x = k // 2, k % 2, s // 2, s % 2
    xo = 1 - x
    barrier = pltpu.get_barrier_semaphore()
    peers = [(s, 2 * y + 1 - c), (2 * z + xo, k)]
    peers += [(s, 2 * lax.rem(y + t, ny) + c) for t in range(1, ny)]
    peers += [(2 * lax.rem(z + t, nz) + x, k) for t in range(1, nz)]
    for peer in peers:
        pl.semaphore_signal(barrier, inc=1, device_id=peer, device_id_type=MESH)
    pl.semaphore_wait(barrier, len(peers))

    def remote(origin, target, sends, recvs, device):
        copy = pltpu.make_async_remote_copy(src_ref=origin, dst_ref=target, send_sem=sends,
                                            recv_sem=recvs, device_id=device, device_id_type=MESH)
        copy.start()
        return copy

    order = [lax.rem(y + t, ny) for t in range(1, ny)] + [y]
    first = [[remote(part.at[2 * yo + 1 - c, :, half], recv1.at[i, h], s1.at[i, h], r1.at[i, h],
                     (s, 2 * y + 1 - c)) for h, half in enumerate((xo, x))] for i, yo in enumerate(order)]
    second = []
    for i, yo in enumerate(order[:-1]):
        for h, half in enumerate((xo, x)):
            first[i][h].wait()
            send2[i, h] = part[2 * yo + c, :, half] + recv1[i, h]
            second.append((i, h, remote(send2.at[i, h], recv2.at[i, h], s2.at[i, h], r2.at[i, h],
                                        (s, 2 * yo + c))))

    def gathered(h, half):
        first[ny - 1][h].wait()
        value = part[2 * y + c, :, half] + recv1[ny - 1, h]
        for i, g, copy in second:
            if g == h:
                copy.wait()
                value = value + recv2[i, h]
        return value

    send3[...] = gathered(0, xo)
    third = remote(send3, recv3, s3, r3, (2 * z + xo, k))
    kept = gathered(1, x)
    third.wait()
    send4[...] = kept + recv3[...]
    last = []
    for t in range(1, nz):
        zo = lax.rem(z + t, nz)
        last.append(remote(send4.at[zo], recv4.at[t - 1], s4.at[t - 1], r4.at[t - 1], (2 * zo + x, k)))
    value = send4[z]
    for i, copy in enumerate(last):
        copy.wait()
        value = value + recv4[i]
    out[...] = value * scale


def fast_shards(n, ns, snapshots, mass_blocks, neighbours, eigvecs):
    block_rows, picks, size, _ = mass_blocks.shape
    total, width = snapshots.shape
    rim = HB * size
    rows = total // n
    snaps = n * width
    sem = pltpu.SemaphoreType.DMA
    ny, nz = n // 2, ns // 2
    ext = pl.pallas_call(
        functools.partial(exchange, n, ns, rim),
        out_shape=jax.ShapeDtypeStruct((n, rows + 2 * rim, width), BF16),
        in_specs=[pl.BlockSpec(memory_space=pl.ANY)],
        out_specs=pl.BlockSpec(memory_space=pl.ANY),
        scratch_shapes=[
            pltpu.VMEM((rows + rim, width), BF16), pltpu.VMEM((rim, width), BF16),
            sem((2,)), sem((2,)), sem, sem,
            sem((ny, 2)), sem((ny, 2)), sem((ny, 2)), sem((ny, 2)), sem((ny, 2)), sem((ny, 2)),
            sem((n,)), sem((n,)), sem((2,)),
        ],
        compiler_params=pltpu.CompilerParams(collective_id=0, has_side_effects=True),
        name="exchange",
    )(snapshots)
    first_block = (lax.axis_index("space") * n + lax.axis_index("snap")) * block_rows
    near = neighbours - first_block + HB
    per_step = 4 if block_rows % 4 == 0 else 1
    modes_count = eigvecs.shape[1]
    weighted, modes, corr = pl.pallas_call(
        functools.partial(compute, n, per_step),
        out_shape=(jax.ShapeDtypeStruct((rows, snaps), BF16),
                   jax.ShapeDtypeStruct((rows, modes_count), BF16),
                   jax.ShapeDtypeStruct((n, snaps, width), F32)),
        grid_spec=pltpu.PrefetchScalarGridSpec(
            num_scalar_prefetch=1,
            grid=(block_rows // per_step,),
            in_specs=[
                pl.BlockSpec(ext.shape, lambda i, near: (0, 0, 0)),
                pl.BlockSpec((per_step, picks, size, size), lambda i, near: (i, 0, 0, 0)),
                pl.BlockSpec(eigvecs.shape, lambda i, near: (0, 0)),
            ],
            out_specs=[
                pl.BlockSpec((per_step * size, snaps), lambda i, near: (i, 0)),
                pl.BlockSpec((per_step * size, modes_count), lambda i, near: (i, 0)),
                pl.BlockSpec((n, snaps, width), lambda i, near: (0, 0, 0)),
            ],
        ),
        compiler_params=pltpu.CompilerParams(vmem_limit_bytes=48 * 2**20),
        name="weigh",
    )(near, ext, mass_blocks, eigvecs)
    tile = snaps // ns
    piece = (nz, tile, width)
    vmem = pltpu.VMEM
    out = pl.pallas_call(
        functools.partial(reduce_kernel, n, ns, 1.0 / (total * ns)),
        out_shape=jax.ShapeDtypeStruct((tile, width), F32),
        in_specs=[pl.BlockSpec(memory_space=pltpu.VMEM)],
        out_specs=pl.BlockSpec(memory_space=pltpu.VMEM),
        scratch_shapes=[
            vmem((ny, 2) + piece, F32), vmem((ny, 2) + piece, F32), vmem((ny, 2) + piece, F32),
            vmem(piece, F32), vmem(piece, F32), vmem(piece, F32), vmem(piece, F32),
            sem((ny, 2)), sem((ny, 2)), sem((ny, 2)), sem((ny, 2)), sem, sem, sem((nz,)), sem((nz,)),
        ],
        compiler_params=pltpu.CompilerParams(collective_id=1, has_side_effects=True),
        name="reduce",
    )(corr.reshape(n, nz, 2, tile, width))
    return weighted, out.T, modes


def shifted(block, axis, distance):
    devices = range(lax.axis_size(axis))
    route = [(i - distance, i) for i in devices if i - distance in devices]
    return lax.ppermute(block, axis, route)


def plain_shards(snapshots, mass_blocks, neighbours, eigvecs):
    local_rows = lax.all_to_all(snapshots, "snap", split_axis=0, concat_axis=1, tiled=True)
    row_count, col_count = local_rows.shape
    block_size = mass_blocks.shape[2]
    rim_rows = HB * block_size
    below_rim = shifted(local_rows[row_count - rim_rows :], ("space", "snap"), 1)
    above_rim = shifted(local_rows[:rim_rows], ("space", "snap"), -1)
    extended = jnp.concatenate([below_rim, local_rows, above_rim], axis=0).reshape(
        -1, block_size, col_count
    )
    first_block = lax.axis_index(("space", "snap")) * (row_count // block_size)
    local_ids = neighbours - first_block + HB
    nearby = extended[local_ids]
    weighted = jnp.einsum("bjrc,bjcs->brs", mass_blocks, nearby, preferred_element_type=jnp.float32)
    weighted = weighted.reshape(row_count, col_count).astype(jnp.bfloat16)
    partial_corr = jnp.dot(weighted.T, local_rows, preferred_element_type=jnp.float32)
    band = lax.psum_scatter(partial_corr, "snap", scatter_dimension=0, tiled=True)
    correlation = lax.psum_scatter(band, "space", scatter_dimension=1, tiled=True)
    cell_total = row_count * lax.axis_size("space") * lax.axis_size("snap")
    correlation = correlation * (1.0 / cell_total)
    modes = jnp.dot(local_rows, eigvecs, preferred_element_type=jnp.float32).astype(jnp.bfloat16)
    return (weighted, correlation, modes)


def solution(mesh):
    n, ns = mesh.shape["snap"], mesh.shape["space"]

    def shards(snapshots, mass_blocks, neighbours, eigvecs):
        width = snapshots.shape[1]
        rows = snapshots.shape[0] // n
        tile = n * width // ns
        whole = width % 128 == 0 and tile % 8 == 0 and n % 2 == 0 and ns % 2 == 0
        if whole and n > 2 and ns > 2 and rows > 2 * HB * mass_blocks.shape[2]:
            return fast_shards(n, ns, snapshots, mass_blocks, neighbours, eigvecs)
        return plain_shards(snapshots, mass_blocks, neighbours, eigvecs)

    in_specs = (
        P("space", "snap"),
        P(("space", "snap"), None, None, None),
        P(("space", "snap"), None),
        P(),
    )
    out_specs = (P(("space", "snap"), None), P("snap", "space"), P(("space", "snap"), None))
    return jax.shard_map(shards, mesh=mesh, in_specs=in_specs, out_specs=out_specs, check_vma=False)
```

```python
import functools

import jax
import jax.numpy as jnp
from jax import lax
from jax.experimental import pallas as pl
from jax.experimental.pallas import tpu as pltpu
from jax.sharding import PartitionSpec as P

HB = 4
MESH = pl.DeviceIdType.MESH
BF16 = jnp.bfloat16
F32 = jnp.float32


def reduce_tiles(n, ns, part, recv1, send2, recv2, send3, recv3, send4, recv4,
                 s1, r1, s2, r2, s3, r3, s4, r4):
    ny, nz = n // 2, ns // 2
    s, k = lax.axis_index("space"), lax.axis_index("snap")
    y, c, z, x = k // 2, k % 2, s // 2, s % 2
    xo = 1 - x

    def remote(origin, target, sends, recvs, device):
        copy = pltpu.make_async_remote_copy(src_ref=origin, dst_ref=target, send_sem=sends,
                                            recv_sem=recvs, device_id=device, device_id_type=MESH)
        copy.start()
        return copy

    order = [lax.rem(y + t, ny) for t in range(1, ny)] + [y]
    first = [[remote(part.at[2 * yo + 1 - c, :, half], recv1.at[i, h], s1.at[i, h], r1.at[i, h],
                     (s, 2 * y + 1 - c)) for h, half in enumerate((xo, x))] for i, yo in enumerate(order)]
    second = []
    for i, yo in enumerate(order[:-1]):
        for h, half in enumerate((xo, x)):
            first[i][h].wait()
            send2[i, h] = part[2 * yo + c, :, half] + recv1[i, h]
            second.append((i, h, remote(send2.at[i, h], recv2.at[i, h], s2.at[i, h], r2.at[i, h],
                                        (s, 2 * yo + c))))

    def gathered(h, half):
        first[ny - 1][h].wait()
        value = part[2 * y + c, :, half] + recv1[ny - 1, h]
        for i, g, copy in second:
            if g == h:
                copy.wait()
                value = value + recv2[i, h]
        return value

    send3[...] = gathered(0, xo)
    third = remote(send3, recv3, s3, r3, (2 * z + xo, k))
    kept = gathered(1, x)
    third.wait()
    send4[...] = kept + recv3[...]
    last = []
    for t in range(1, nz):
        zo = lax.rem(z + t, nz)
        last.append(remote(send4.at[zo], recv4.at[t - 1], s4.at[t - 1], r4.at[t - 1], (2 * zo + x, k)))
    value = send4[z]
    for i, copy in enumerate(last):
        copy.wait()
        value = value + recv4[i]
    return value


def fused(n, ns, size, scale, near, src, mass_hbm, eig, weighted_hbm, modes_hbm, corr_out,
          ext, win, mass, weighted, modes, part, loc, own_sems, out_sems,
          send_mid, recv_mid, send_main, recv_main, send_fwd, recv_fwd,
          send_rim, recv_rim, send_out, *reduce_refs):
    ny, nz = n // 2, ns // 2
    s, k = lax.axis_index("space"), lax.axis_index("snap")
    y, c, z, x = k // 2, k % 2, s // 2, s % 2
    partner = 2 * y + 1 - c
    rim = HB * size
    total = src.shape[0]
    chip_rows = total // ny
    rows = chip_rows // 2
    pieces = rows // rim
    width = src.shape[1]

    barrier = pltpu.get_barrier_semaphore()
    for t in range(1, n):
        pl.semaphore_signal(barrier, inc=1, device_id=(s, lax.rem(k + t, n)), device_id_type=MESH)
    for t in range(1, nz):
        pl.semaphore_signal(barrier, inc=1, device_id=(2 * lax.rem(z + t, nz) + x, k), device_id_type=MESH)

    @pl.when(s > 0)
    def _():
        for t in range(n):
            pl.semaphore_signal(barrier, inc=1, device_id=(s - 1, t), device_id_type=MESH)

    @pl.when(s < ns - 1)
    def _():
        for t in range(n):
            pl.semaphore_signal(barrier, inc=1, device_id=(s + 1, t), device_id_type=MESH)

    def rows_of(first, count):
        return src.at[pl.ds(first, count)]

    keep = pltpu.make_async_copy(rows_of(y * chip_rows + c * (rows - rim), rows + rim),
                                 ext.at[k, pl.ds((1 - c) * rim, rows + rim)], loc.at[0])
    keep.start()
    inner = (k > 0) & (k < n - 1)
    edge_row = jnp.where(inner, jnp.where(c == 0, y * chip_rows - rim, (y + 1) * chip_rows), 0)
    edge_keep = pltpu.make_async_copy(rows_of(edge_row, rim), ext.at[k, pl.ds(c * (rows + rim), rim)],
                                      loc.at[1])
    pl.when(inner)(edge_keep.start)
    fetch = pltpu.make_async_copy(mass_hbm, mass, loc.at[2])
    fetch.start()
    part[...] = jnp.zeros_like(part)

    sides = jnp.where(s > 0, 1, 0) + jnp.where(s < ns - 1, 1, 0)
    pl.semaphore_wait(barrier, n - 1 + nz - 1 + n * sides)

    def remote(origin, slab, to_row, count, sends, recvs, device):
        return pltpu.make_async_remote_copy(
            src_ref=origin, dst_ref=ext.at[slab, pl.ds(to_row, count)],
            send_sem=sends, recv_sem=recvs, device_id=device, device_id_type=MESH)

    mids, mains = [], []
    for t in range(1, ny):
        yo = lax.rem(y + t, ny)
        base = yo * chip_rows
        for co in range(2):
            mids.append(remote(rows_of(base + rows - rim + co * rim, rim), k, rows if co == 0 else rim, rim,
                               send_mid.at[t, co], recv_mid.at[t, c], (s, 2 * yo + co)))
    for p in range(pieces - 1):
        for t in range(1, ny):
            yo = lax.rem(y + t, ny)
            base = yo * chip_rows
            for co in range(2):
                first = (pieces - 2 - p) * rim if co == 0 else rows + (1 + p) * rim
                to = (pieces - 1 - p) * rim if co == 0 else (2 + p) * rim
                mains.append(remote(rows_of(base + first, rim), k, to, rim, send_main.at[t, co, p],
                                    recv_main.at[t, c, p], (s, 2 * yo + co)))
    own = remote(rows_of(y * chip_rows + (1 - c) * (rows - rim), rows + rim), k, c * rim, rows + rim,
                 own_sems.at[0], own_sems.at[1], (s, partner))
    down = remote(rows_of(0, rim), k, rows + rim, rim, send_out.at[0], recv_rim.at[k], (s - 1, n - 1))
    up = remote(rows_of(total - rim, rim), k, 0, rim, send_out.at[1], recv_rim.at[k], (s + 1, 0))

    for copy in mids:
        copy.start()
    own.start()
    pl.when(s > 0)(down.start)
    pl.when(s < ns - 1)(up.start)
    edges = []
    for target in range(1, n - 1):
        low = target % 2 == 0
        first = (target // 2) * chip_rows - rim if low else (target // 2 + 1) * chip_rows
        edge = remote(rows_of(first, rim), k, 0 if low else rows + rim, rim,
                      send_rim.at[target], recv_rim.at[k], (s, target))
        edges.append((target, edge))
        pl.when(k != target)(edge.start)
    for copy in mains:
        copy.start()

    def wait_for(slab, to_row, count, recvs):
        remote(ext.at[slab, pl.ds(to_row, count)], slab, to_row, count, own_sems.at[0], recvs,
               (s, partner)).wait_recv()

    forwards = []
    at, to = (1 - c) * rows + c * rim, (1 - c) * (rows + rim)
    for t in range(1, ny):
        for co in range(2):
            slab = 2 * lax.rem(y + ny - t, ny) + co
            wait_for(slab, at, rim, recv_mid.at[t, co])
            forward = remote(ext.at[slab, pl.ds(at, rim)], slab, c * (rows + rim), rim,
                             send_fwd.at[t, co], recv_fwd.at[t, co], (s, partner))
            forward.start()
            forwards.append((slab, t, co, forward))
    keep.wait()
    wait_for(partner, (1 - c) * rim, rows + rim, own_sems.at[1])
    for slab, t, co, forward in forwards:
        wait_for(slab, to, rim, recv_fwd.at[t, co])
    fetch.wait()

    def slot_of(order):
        return jnp.where(c == 1, order, pieces + 1 - order)

    def admit(order):
        slot = slot_of(order)
        place = lax.rem(slot, 3) * HB
        for slab in range(n):
            held = ext[slab, pl.ds(pl.multiple_of(slot * rim, rim), rim), :]
            win[pl.ds(place, HB), :, slab * width:(slab + 1) * width] = held.reshape(HB, size, width)

    def out_copies(group):
        first = pl.multiple_of((slot_of(group + 1) - 1) * rim, rim)
        return [pltpu.make_async_copy(held.at[pl.ds(first, rim)], target.at[pl.ds(first, rim)],
                                      out_sems.at[i, group])
                for i, (held, target) in enumerate(((weighted, weighted_hbm), (modes, modes_hbm)))]

    def work(group):
        slot = slot_of(group + 1)
        first = pl.multiple_of((slot - 1) * rim, rim)
        for i in range(HB):
            row = (slot - 1) * HB + i
            masses = jnp.concatenate([mass[row, j] for j in range(mass.shape[1])], axis=1)
            fields = jnp.concatenate(
                [win[near[row, j]] for j in range(mass.shape[1])], axis=0)
            product = jnp.dot(masses, fields, preferred_element_type=F32)
            weighted[pl.ds(pl.multiple_of(first + i * size, size), size), :] = product.astype(BF16)
        here = win[pl.ds(lax.rem(slot, 3) * HB, HB)].reshape(rim, n * width)
        modes[pl.ds(first, rim), :] = jnp.dot(here, eig[...], preferred_element_type=F32).astype(BF16)
        sums = lax.dot_general(here, weighted[pl.ds(first, rim), :], (((0,), (0,)), ((), ())),
                               preferred_element_type=F32)
        tile = part.shape[3]
        for band in range(n):
            for index in range(ns):
                part[band, index // 2, index % 2] += sums[index * tile:(index + 1) * tile,
                                                          band * width:(band + 1) * width]
        for copy in out_copies(group):
            copy.start()

    admit(0)
    admit(1)

    @pl.loop(0, pieces - 1)
    def _(p):
        place = pl.multiple_of(slot_of(p + 2) * rim, rim)
        for slab, t, co, forward in forwards:
            wait_for(slab, place, rim, recv_main.at[t, co, p])
        admit(p + 2)
        work(p)

    lowest = (k == 0) & (s == 0)
    highest = (k == n - 1) & (s == ns - 1)
    pl.when(inner)(edge_keep.wait)
    for slab in range(n):
        expected = jnp.logical_not(lowest | highest | (inner & (k == slab)))

        @pl.when(expected)
        def _(slab=slab):
            wait_for(slab, c * (rows + rim), rim, recv_rim.at[slab])
    admit(pieces + 1)
    work(pieces - 1)

    corr_out[...] = reduce_tiles(n, ns, part, *reduce_refs) * scale

    for copy in mids + mains + [own] + [entry[3] for entry in forwards]:
        copy.wait_send()
    pl.when(s > 0)(down.wait_send)
    pl.when(s < ns - 1)(up.wait_send)
    for target, edge in edges:
        pl.when(k != target)(edge.wait_send)

    @pl.loop(0, pieces)
    def _(group):
        for copy in out_copies(group):
            copy.wait()


def fast_shards(n, ns, snapshots, mass_blocks, neighbours, eigvecs):
    block_rows, picks, size, _ = mass_blocks.shape
    total, width = snapshots.shape
    rim = HB * size
    rows = total // n
    snaps = n * width
    pieces = rows // rim
    sem = pltpu.SemaphoreType.DMA
    vmem = pltpu.VMEM
    ny, nz = n // 2, ns // 2
    tile = snaps // ns
    piece = (nz, tile, width)
    first_block = (lax.axis_index("space") * n + lax.axis_index("snap")) * block_rows
    near = lax.rem(neighbours - first_block + HB, 3 * HB)
    modes_count = eigvecs.shape[1]
    anywhere = pl.BlockSpec(memory_space=pl.ANY)
    weighted, modes, corr = pl.pallas_call(
        functools.partial(fused, n, ns, size, 1.0 / (total * ns)),
        out_shape=(jax.ShapeDtypeStruct((rows, snaps), BF16),
                   jax.ShapeDtypeStruct((rows, modes_count), BF16),
                   jax.ShapeDtypeStruct((tile, width), F32)),
        in_specs=[pl.BlockSpec(memory_space=pltpu.SMEM), anywhere, anywhere,
                  pl.BlockSpec(memory_space=pltpu.VMEM)],
        out_specs=(anywhere, anywhere, pl.BlockSpec(memory_space=pltpu.VMEM)),
        scratch_shapes=[
            vmem((n, rows + 2 * rim, width), BF16), vmem((3 * HB, size, snaps), BF16),
            vmem(mass_blocks.shape, BF16), vmem((rows, snaps), BF16), vmem((rows, modes_count), BF16),
            vmem((n, nz, 2, tile, width), F32),
            sem((3,)), sem((2,)), sem((2, pieces)),
            sem((ny, 2)), sem((ny, 2)), sem((ny, 2, pieces - 1)), sem((ny, 2, pieces - 1)),
            sem((ny, 2)), sem((ny, 2)), sem((n,)), sem((n,)), sem((2,)),
            vmem((ny, 2) + piece, F32), vmem((ny, 2) + piece, F32), vmem((ny, 2) + piece, F32),
            vmem(piece, F32), vmem(piece, F32), vmem(piece, F32), vmem(piece, F32),
            sem((ny, 2)), sem((ny, 2)), sem((ny, 2)), sem((ny, 2)), sem, sem, sem((nz,)), sem((nz,)),
        ],
        compiler_params=pltpu.CompilerParams(collective_id=0, has_side_effects=True,
                                             vmem_limit_bytes=62 * 2**20),
        name="fused",
    )(near, snapshots, mass_blocks, eigvecs)
    return weighted, corr.T, modes


def shifted(block, axis, distance):
    devices = range(lax.axis_size(axis))
    route = [(i - distance, i) for i in devices if i - distance in devices]
    return lax.ppermute(block, axis, route)


def plain_shards(snapshots, mass_blocks, neighbours, eigvecs):
    local_rows = lax.all_to_all(snapshots, "snap", split_axis=0, concat_axis=1, tiled=True)
    row_count, col_count = local_rows.shape
    block_size = mass_blocks.shape[2]
    rim_rows = HB * block_size
    below_rim = shifted(local_rows[row_count - rim_rows :], ("space", "snap"), 1)
    above_rim = shifted(local_rows[:rim_rows], ("space", "snap"), -1)
    extended = jnp.concatenate([below_rim, local_rows, above_rim], axis=0).reshape(
        -1, block_size, col_count
    )
    first_block = lax.axis_index(("space", "snap")) * (row_count // block_size)
    local_ids = neighbours - first_block + HB
    nearby = extended[local_ids]
    weighted = jnp.einsum("bjrc,bjcs->brs", mass_blocks, nearby, preferred_element_type=jnp.float32)
    weighted = weighted.reshape(row_count, col_count).astype(jnp.bfloat16)
    partial_corr = jnp.dot(weighted.T, local_rows, preferred_element_type=jnp.float32)
    band = lax.psum_scatter(partial_corr, "snap", scatter_dimension=0, tiled=True)
    correlation = lax.psum_scatter(band, "space", scatter_dimension=1, tiled=True)
    cell_total = row_count * lax.axis_size("space") * lax.axis_size("snap")
    correlation = correlation * (1.0 / cell_total)
    modes = jnp.dot(local_rows, eigvecs, preferred_element_type=jnp.float32).astype(jnp.bfloat16)
    return (weighted, correlation, modes)


def solution(mesh):
    n, ns = mesh.shape["snap"], mesh.shape["space"]

    def shards(snapshots, mass_blocks, neighbours, eigvecs):
        width = snapshots.shape[1]
        rows = snapshots.shape[0] // n
        tile = n * width // ns
        rim = HB * mass_blocks.shape[2]
        whole = width % 128 == 0 and tile % 8 == 0 and n % 2 == 0 and ns % 2 == 0
        if whole and n > 2 and ns > 2 and rows % rim == 0 and rows > 2 * rim:
            return fast_shards(n, ns, snapshots, mass_blocks, neighbours, eigvecs)
        return plain_shards(snapshots, mass_blocks, neighbours, eigvecs)

    in_specs = (
        P("space", "snap"),
        P(("space", "snap"), None, None, None),
        P(("space", "snap"), None),
        P(),
    )
    out_specs = (P(("space", "snap"), None), P("snap", "space"), P(("space", "snap"), None))
    return jax.shard_map(shards, mesh=mesh, in_specs=in_specs, out_specs=out_specs, check_vma=False)
```

```python
import functools

import jax
import jax.numpy as jnp
from jax import lax
from jax.experimental import pallas as pl
from jax.experimental.pallas import tpu as pltpu
from jax.sharding import PartitionSpec as P

HB = 4
MESH = pl.DeviceIdType.MESH
BF16 = jnp.bfloat16
F32 = jnp.float32


def reduce_tiles(n, ns, part, recv1, send2, recv2, send3, recv3, send4, recv4,
                 s1, r1, s2, r2, s3, r3, s4, r4):
    ny, nz = n // 2, ns // 2
    s, k = lax.axis_index("space"), lax.axis_index("snap")
    y, c, z, x = k // 2, k % 2, s // 2, s % 2
    xo = 1 - x

    def remote(origin, target, sends, recvs, device):
        copy = pltpu.make_async_remote_copy(src_ref=origin, dst_ref=target, send_sem=sends,
                                            recv_sem=recvs, device_id=device, device_id_type=MESH)
        copy.start()
        return copy

    order = [lax.rem(y + t, ny) for t in range(1, ny)] + [y]
    first = [[remote(part.at[2 * yo + 1 - c, :, half], recv1.at[i, h], s1.at[i, h], r1.at[i, h],
                     (s, 2 * y + 1 - c)) for h, half in enumerate((xo, x))] for i, yo in enumerate(order)]
    second = []
    for i, yo in enumerate(order[:-1]):
        for h, half in enumerate((xo, x)):
            first[i][h].wait()
            send2[i, h] = part[2 * yo + c, :, half] + recv1[i, h]
            second.append((i, h, remote(send2.at[i, h], recv2.at[i, h], s2.at[i, h], r2.at[i, h],
                                        (s, 2 * yo + c))))

    def gathered(h, half):
        first[ny - 1][h].wait()
        value = part[2 * y + c, :, half] + recv1[ny - 1, h]
        for i, g, copy in second:
            if g == h:
                copy.wait()
                value = value + recv2[i, h]
        return value

    send3[...] = gathered(0, xo)
    third = remote(send3, recv3, s3, r3, (2 * z + xo, k))
    kept = gathered(1, x)
    third.wait()
    send4[...] = kept + recv3[...]
    last = []
    for t in range(1, nz):
        zo = lax.rem(z + t, nz)
        last.append(remote(send4.at[zo], recv4.at[t - 1], s4.at[t - 1], r4.at[t - 1], (2 * zo + x, k)))
    value = send4[z]
    for i, copy in enumerate(last):
        copy.wait()
        value = value + recv4[i]
    return value


def fused(n, ns, size, scale, near, src, mass_hbm, eig, weighted_hbm, modes_hbm, corr_out,
          ext, win, mass, weighted, modes, part, loc, own_sems, out_sems,
          send_mid, recv_mid, send_main, recv_main, send_fwd, recv_fwd,
          send_rim, recv_rim, send_out, *reduce_refs):
    ny, nz = n // 2, ns // 2
    s, k = lax.axis_index("space"), lax.axis_index("snap")
    y, c, z, x = k // 2, k % 2, s // 2, s % 2
    partner = 2 * y + 1 - c
    rim = HB * size
    total = src.shape[0]
    chip_rows = total // ny
    rows = chip_rows // 2
    pieces = rows // rim
    width = src.shape[1]

    barrier = pltpu.get_barrier_semaphore()
    for t in range(1, n):
        pl.semaphore_signal(barrier, inc=1, device_id=(s, lax.rem(k + t, n)), device_id_type=MESH)
    for t in range(1, nz):
        pl.semaphore_signal(barrier, inc=1, device_id=(2 * lax.rem(z + t, nz) + x, k), device_id_type=MESH)

    @pl.when(s > 0)
    def _():
        for t in range(n):
            pl.semaphore_signal(barrier, inc=1, device_id=(s - 1, t), device_id_type=MESH)

    @pl.when(s < ns - 1)
    def _():
        for t in range(n):
            pl.semaphore_signal(barrier, inc=1, device_id=(s + 1, t), device_id_type=MESH)

    def rows_of(first, count):
        return src.at[pl.ds(first, count)]

    keep = pltpu.make_async_copy(rows_of(y * chip_rows + c * (rows - rim), rows + rim),
                                 ext.at[k, pl.ds((1 - c) * rim, rows + rim)], loc.at[0])
    keep.start()
    inner = (k > 0) & (k < n - 1)
    edge_row = jnp.where(inner, jnp.where(c == 0, y * chip_rows - rim, (y + 1) * chip_rows), 0)
    edge_keep = pltpu.make_async_copy(rows_of(edge_row, rim), ext.at[k, pl.ds(c * (rows + rim), rim)],
                                      loc.at[1])
    pl.when(inner)(edge_keep.start)
    fetch = pltpu.make_async_copy(mass_hbm, mass, loc.at[2])
    fetch.start()
    part[...] = jnp.zeros_like(part)

    sides = jnp.where(s > 0, 1, 0) + jnp.where(s < ns - 1, 1, 0)
    pl.semaphore_wait(barrier, n - 1 + nz - 1 + n * sides)

    def remote(origin, slab, to_row, count, sends, recvs, device):
        return pltpu.make_async_remote_copy(
            src_ref=origin, dst_ref=ext.at[slab, pl.ds(to_row, count)],
            send_sem=sends, recv_sem=recvs, device_id=device, device_id_type=MESH)

    mids, mains = [], []
    for t in range(1, ny):
        yo = lax.rem(y + t, ny)
        base = yo * chip_rows
        for co in range(2):
            mids.append(remote(rows_of(base + rows - rim + co * rim, rim), k, rows if co == 0 else rim, rim,
                               send_mid.at[t, co], recv_mid.at[t, c], (s, 2 * yo + co)))
    for p in range(pieces - 1):
        for t in range(1, ny):
            yo = lax.rem(y + t, ny)
            base = yo * chip_rows
            for co in range(2):
                first = (pieces - 2 - p) * rim if co == 0 else rows + (1 + p) * rim
                to = (pieces - 1 - p) * rim if co == 0 else (2 + p) * rim
                mains.append(remote(rows_of(base + first, rim), k, to, rim, send_main.at[t, co, p],
                                    recv_main.at[t, c, p], (s, 2 * yo + co)))
    own = remote(rows_of(y * chip_rows + (1 - c) * (rows - rim), rows + rim), k, c * rim, rows + rim,
                 own_sems.at[0], own_sems.at[1], (s, partner))
    down = remote(rows_of(0, rim), k, rows + rim, rim, send_out.at[0], recv_rim.at[k], (s - 1, n - 1))
    up = remote(rows_of(total - rim, rim), k, 0, rim, send_out.at[1], recv_rim.at[k], (s + 1, 0))

    for copy in mids:
        copy.start()
    own.start()
    pl.when(s > 0)(down.start)
    pl.when(s < ns - 1)(up.start)
    edges = []
    for target in range(1, n - 1):
        low = target % 2 == 0
        first = (target // 2) * chip_rows - rim if low else (target // 2 + 1) * chip_rows
        edge = remote(rows_of(first, rim), k, 0 if low else rows + rim, rim,
                      send_rim.at[target], recv_rim.at[k], (s, target))
        edges.append((target, edge))
        pl.when(k != target)(edge.start)
    for copy in mains:
        copy.start()

    def wait_for(slab, to_row, count, recvs):
        remote(ext.at[slab, pl.ds(to_row, count)], slab, to_row, count, own_sems.at[0], recvs,
               (s, partner)).wait_recv()

    forwards = []
    at, to = (1 - c) * rows + c * rim, (1 - c) * (rows + rim)
    for t in range(1, ny):
        for co in range(2):
            slab = 2 * lax.rem(y + ny - t, ny) + co
            wait_for(slab, at, rim, recv_mid.at[t, co])
            forward = remote(ext.at[slab, pl.ds(at, rim)], slab, c * (rows + rim), rim,
                             send_fwd.at[t, co], recv_fwd.at[t, co], (s, partner))
            forward.start()
            forwards.append((slab, t, co, forward))
    keep.wait()
    wait_for(partner, (1 - c) * rim, rows + rim, own_sems.at[1])
    for slab, t, co, forward in forwards:
        wait_for(slab, to, rim, recv_fwd.at[t, co])
    fetch.wait()

    def slot_of(order):
        return jnp.where(c == 1, order, pieces + 1 - order)

    def admit(order):
        slot = slot_of(order)
        place = lax.rem(slot, 3) * HB
        for slab in range(n):
            held = ext[slab, pl.ds(pl.multiple_of(slot * rim, rim), rim), :]
            win[pl.ds(place, HB), :, slab * width:(slab + 1) * width] = held.reshape(HB, size, width)

    def out_copies(group):
        first = pl.multiple_of((slot_of(group + 1) - 1) * rim, rim)
        return [pltpu.make_async_copy(held.at[pl.ds(first, rim)], target.at[pl.ds(first, rim)],
                                      out_sems.at[i, group])
                for i, (held, target) in enumerate(((weighted, weighted_hbm), (modes, modes_hbm)))]

    def work(group):
        slot = slot_of(group + 1)
        first = pl.multiple_of((slot - 1) * rim, rim)
        for i in range(HB):
            row = (slot - 1) * HB + i
            masses = jnp.concatenate([mass[row, j] for j in range(mass.shape[1])], axis=1)
            fields = jnp.concatenate(
                [win[near[row, j]] for j in range(mass.shape[1])], axis=0)
            product = jnp.dot(masses, fields, preferred_element_type=F32)
            weighted[pl.ds(pl.multiple_of(first + i * size, size), size), :] = product.astype(BF16)
        here = win[pl.ds(lax.rem(slot, 3) * HB, HB)].reshape(rim, n * width)
        modes[pl.ds(first, rim), :] = jnp.dot(here, eig[...], preferred_element_type=F32).astype(BF16)
        sums = lax.dot_general(here, weighted[pl.ds(first, rim), :], (((0,), (0,)), ((), ())),
                               preferred_element_type=F32)
        tile = part.shape[3]
        for band in range(n):
            for index in range(ns):
                part[band, index // 2, index % 2] += sums[index * tile:(index + 1) * tile,
                                                          band * width:(band + 1) * width]
        for copy in out_copies(group):
            copy.start()

    admit(0)
    admit(1)

    @pl.loop(0, pieces - 1)
    def _(p):
        place = pl.multiple_of(slot_of(p + 2) * rim, rim)
        for slab, t, co, forward in forwards:
            wait_for(slab, place, rim, recv_main.at[t, co, p])
        admit(p + 2)
        work(p)

    lowest = (k == 0) & (s == 0)
    highest = (k == n - 1) & (s == ns - 1)
    pl.when(inner)(edge_keep.wait)
    for slab in range(n):
        expected = jnp.logical_not(lowest | highest | (inner & (k == slab)))

        @pl.when(expected)
        def _(slab=slab):
            wait_for(slab, c * (rows + rim), rim, recv_rim.at[slab])
    admit(pieces + 1)
    work(pieces - 1)

    corr_out[...] = reduce_tiles(n, ns, part, *reduce_refs) * scale

    for copy in mids + mains + [own] + [entry[3] for entry in forwards]:
        copy.wait_send()
    pl.when(s > 0)(down.wait_send)
    pl.when(s < ns - 1)(up.wait_send)
    for target, edge in edges:
        pl.when(k != target)(edge.wait_send)

    @pl.loop(0, pieces)
    def _(group):
        for copy in out_copies(group):
            copy.wait()


def fast_shards(n, ns, snapshots, mass_blocks, neighbours, eigvecs):
    block_rows, picks, size, _ = mass_blocks.shape
    total, width = snapshots.shape
    rim = HB * size
    rows = total // n
    snaps = n * width
    pieces = rows // rim
    sem = pltpu.SemaphoreType.DMA
    vmem = pltpu.VMEM
    ny, nz = n // 2, ns // 2
    tile = snaps // ns
    piece = (nz, tile, width)
    first_block = (lax.axis_index("space") * n + lax.axis_index("snap")) * block_rows
    near = lax.rem(neighbours - first_block + HB, 3 * HB)
    modes_count = eigvecs.shape[1]
    anywhere = pl.BlockSpec(memory_space=pl.ANY)
    weighted, modes, corr = pl.pallas_call(
        functools.partial(fused, n, ns, size, 1.0 / (total * ns)),
        out_shape=(jax.ShapeDtypeStruct((rows, snaps), BF16),
                   jax.ShapeDtypeStruct((rows, modes_count), BF16),
                   jax.ShapeDtypeStruct((tile, width), F32)),
        in_specs=[pl.BlockSpec(memory_space=pltpu.SMEM), anywhere, anywhere,
                  pl.BlockSpec(memory_space=pltpu.VMEM)],
        out_specs=(anywhere, anywhere, pl.BlockSpec(memory_space=pltpu.VMEM)),
        scratch_shapes=[
            vmem((n, rows + 2 * rim, width), BF16), vmem((3 * HB, size, snaps), BF16),
            vmem(mass_blocks.shape, BF16), vmem((rows, snaps), BF16), vmem((rows, modes_count), BF16),
            vmem((n, nz, 2, tile, width), F32),
            sem((3,)), sem((2,)), sem((2, pieces)),
            sem((ny, 2)), sem((ny, 2)), sem((ny, 2, pieces - 1)), sem((ny, 2, pieces - 1)),
            sem((ny, 2)), sem((ny, 2)), sem((n,)), sem((n,)), sem((2,)),
            vmem((ny, 2) + piece, F32), vmem((ny, 2) + piece, F32), vmem((ny, 2) + piece, F32),
            vmem(piece, F32), vmem(piece, F32), vmem(piece, F32), vmem(piece, F32),
            sem((ny, 2)), sem((ny, 2)), sem((ny, 2)), sem((ny, 2)), sem, sem, sem((nz,)), sem((nz,)),
        ],
        compiler_params=pltpu.CompilerParams(collective_id=0, has_side_effects=True,
                                             vmem_limit_bytes=40 * 2**20),
        name="fused",
    )(near, pltpu.with_memory_space_constraint(snapshots, pltpu.HBM), pltpu.with_memory_space_constraint(mass_blocks, pltpu.HBM), eigvecs)
    return weighted, corr.T, modes


def shifted(block, axis, distance):
    devices = range(lax.axis_size(axis))
    route = [(i - distance, i) for i in devices if i - distance in devices]
    return lax.ppermute(block, axis, route)


def plain_shards(snapshots, mass_blocks, neighbours, eigvecs):
    local_rows = lax.all_to_all(snapshots, "snap", split_axis=0, concat_axis=1, tiled=True)
    row_count, col_count = local_rows.shape
    block_size = mass_blocks.shape[2]
    rim_rows = HB * block_size
    below_rim = shifted(local_rows[row_count - rim_rows :], ("space", "snap"), 1)
    above_rim = shifted(local_rows[:rim_rows], ("space", "snap"), -1)
    extended = jnp.concatenate([below_rim, local_rows, above_rim], axis=0).reshape(
        -1, block_size, col_count
    )
    first_block = lax.axis_index(("space", "snap")) * (row_count // block_size)
    local_ids = neighbours - first_block + HB
    nearby = extended[local_ids]
    weighted = jnp.einsum("bjrc,bjcs->brs", mass_blocks, nearby, preferred_element_type=jnp.float32)
    weighted = weighted.reshape(row_count, col_count).astype(jnp.bfloat16)
    partial_corr = jnp.dot(weighted.T, local_rows, preferred_element_type=jnp.float32)
    band = lax.psum_scatter(partial_corr, "snap", scatter_dimension=0, tiled=True)
    correlation = lax.psum_scatter(band, "space", scatter_dimension=1, tiled=True)
    cell_total = row_count * lax.axis_size("space") * lax.axis_size("snap")
    correlation = correlation * (1.0 / cell_total)
    modes = jnp.dot(local_rows, eigvecs, preferred_element_type=jnp.float32).astype(jnp.bfloat16)
    return (weighted, correlation, modes)


def solution(mesh):
    n, ns = mesh.shape["snap"], mesh.shape["space"]

    def shards(snapshots, mass_blocks, neighbours, eigvecs):
        width = snapshots.shape[1]
        rows = snapshots.shape[0] // n
        tile = n * width // ns
        rim = HB * mass_blocks.shape[2]
        whole = width % 128 == 0 and tile % 8 == 0 and n % 2 == 0 and ns % 2 == 0
        if whole and n > 2 and ns > 2 and rows % rim == 0 and rows > 2 * rim:
            return fast_shards(n, ns, snapshots, mass_blocks, neighbours, eigvecs)
        return plain_shards(snapshots, mass_blocks, neighbours, eigvecs)

    in_specs = (
        P("space", "snap"),
        P(("space", "snap"), None, None, None),
        P(("space", "snap"), None),
        P(),
    )
    out_specs = (P(("space", "snap"), None), P("snap", "space"), P(("space", "snap"), None))
    return jax.shard_map(shards, mesh=mesh, in_specs=in_specs, out_specs=out_specs, check_vma=False)
```
